32 devices in a mesh: seq: 8 (over z, x), ch: 4 (over y, core).
Axes of the slice: x: 2, y: 2, z: 4, core: 2. Of those that a mesh axis runs over, the one named last changes fastest.
Arguments:
- features: float32 [1536, 4096], P('ch', 'seq'), may hold values from -6 to 6
- gain_one: float32 [1536], P('ch'), may hold values from 0.5 to 2
- shift_one: float32 [1536], P('ch'), may hold values from -1 to 1
- wide_one: float32 [5, 1536, 1536], P(None, 'ch'), may hold values from -0.0625 to 0.0625
- gain_two: float32 [1536], P('ch'), may hold values from 0.5 to 2
- shift_two: float32 [1536], P('ch'), may hold values from -1 to 1
- wide_two: float32 [5, 1536, 1536], P(None, 'ch'), may hold values from -0.0625 to 0.0625
Outputs:
- regrouped: float32 [8, 384, 512], P('seq', 'ch')
The draws below stay inside these ranges and needn't reach their ends.
All inputs are finite; a program needn't handle non-finite values.
Results may differ from the reference program's by a relative error of at most 0.0001.
Values sent between devices are 32-bit elements; how exact they have to be, the bound alone decides.
No kernel may reach another device: no remote copies, remote signals or barrier semaphores. Data moves between devices by JAX's collectives and lax.ppermute only.
A program may use at most 128 MiB of HBM per device.

```python
import math
import jax
import jax.numpy as jnp
from jax import lax

C = 1536
KW = 5
GROUP = 4
ROWS = 512
LEN = 4096
CHAN_PART = 96
N_SEQ = 8
N_CH = 4


def steps_of(rng, shape, pieces, smallest, top_value):
    def one(position, parts):
        heights = jax.random.uniform(jax.random.fold_in(jax.random.fold_in(rng, 6), position), (parts,), jnp.float32, smallest / len(pieces), top_value / len(pieces))
        return jnp.repeat(jnp.exp(heights), shape[position] // parts).reshape((-1,) + (1,) * (len(shape) - position - 1))

    factor_of = one(*pieces[0])
    for cut in pieces[1:]:
        factor_of = factor_of * one(*cut)
    return factor_of


def scatter_about(rng, dims, width, limit, pieces=(), held_as=jnp.bfloat16):
    drawn = jax.random.normal(rng, dims, jnp.float32) * width
    if len(pieces) > 0:
        drawn = steps_of(rng, dims, pieces, -0.22, 0.18) * drawn
    return jnp.clip(drawn, min=-limit, max=limit).astype(held_as)


def setup_inputs(seed: int = 0) -> dict:
    seeds = jax.random.split(jax.random.key(seed), 8)
    return {
        "features": scatter_about(seeds[0], (C, LEN), 1.0, 6.0, ((0, 4), (1, 8)), jnp.float32),
        "gain_one": jnp.clip(jnp.exp(math.log(2.0) - 1.3862944 * jax.random.uniform(seeds[1], (C,), jnp.float32) ** steps_of(seeds[1], (C,), ((0, 4),), -0.2, 0.2)), 0.5, 2.0),
        "shift_one": jnp.clip(jax.random.uniform(seeds[2], (C,), jnp.float32, -1.0, 1.0) * steps_of(seeds[2], (C,), ((0, 4),), -0.4, 0.0), -1.0, 1.0),
        "wide_one": scatter_about(seeds[3], (KW, C, C), (KW * C) ** -0.5, 0.0625, ((1, 4),), jnp.float32),
        "gain_two": jnp.clip(jnp.exp(math.log(2.0) - 1.3862944 * jax.random.uniform(seeds[4], (C,), jnp.float32) ** steps_of(seeds[4], (C,), ((0, 4),), -0.2, 0.2)), 0.5, 2.0),
        "shift_two": jnp.clip(jax.random.uniform(seeds[5], (C,), jnp.float32, -1.0, 1.0) * steps_of(seeds[5], (C,), ((0, 4),), -0.4, 0.0), -1.0, 1.0),
        "wide_two": scatter_about(seeds[6], (KW, C, C), (KW * C) ** -0.5, 0.0625, ((1, 4),), jnp.float32),
    }


def activate(values, gain, offset):
    return jax.nn.gelu(values * gain[:, None] + offset[:, None], approximate=False)


def convolve(active, weight):
    length = active.shape[1]
    padded = jnp.pad(active, ((0, 0), (2, 2)))
    total = jnp.zeros((weight.shape[2], length), jnp.float32)
    for kernel_tap in range(KW):
        window = padded[:, kernel_tap:kernel_tap + length]
        total = total + jnp.einsum("io,il->ol", weight[kernel_tap], window, precision=lax.Precision.HIGHEST, preferred_element_type=jnp.float32)
    return total


def pool_pairs(values):
    return jnp.max(values.reshape(values.shape[0], values.shape[1] // 2, 2), axis=2)


def reference(features, gain_one, shift_one, wide_one, gain_two, shift_two, wide_two):
    pooled_one = pool_pairs(convolve(activate(features, gain_one, shift_one), wide_one))
    pooled_two = pool_pairs(convolve(activate(pooled_one, gain_two, shift_two), wide_two))
    groups = N_SEQ // GROUP
    split = pooled_two.reshape(N_CH, GROUP, CHAN_PART, groups, ROWS)
    moved = jnp.transpose(split, (3, 1, 0, 2, 4))
    return moved.reshape(N_SEQ, N_CH * CHAN_PART, ROWS)
```

```python
import functools

import jax
import jax.numpy as jnp
from jax import lax
from jax.experimental import pallas as pl
from jax.experimental.pallas import tpu as pltpu
from jax.sharding import PartitionSpec as P

KW = 5
GROUP = 4
EDGE = 8
CHUNK = 264
LANES = 128
VMEM_LIMIT = 2 * 1024 * 1024
VECTORS = pl.BlockSpec(memory_space=pltpu.VMEM)
SCALARS = pl.BlockSpec(memory_space=pltpu.SMEM)
IN_HBM = pl.BlockSpec(memory_space=pltpu.HBM)
LIGHT = 10_000_000_000


def f32(*shape):
    return jax.ShapeDtypeStruct(shape, jnp.float32)


def bf16(*shape):
    return jax.ShapeDtypeStruct(shape, jnp.bfloat16)


def in_hbm(array):
    return pltpu.with_memory_space_constraint(array, pltpu.HBM)


def cost(flops):
    return pl.CostEstimate(flops=flops, transcendentals=0, bytes_accessed=0)


def call(kernel, name, where, args, outs, scratch=(), flops=LIGHT):
    return pl.pallas_call(
        kernel,
        in_specs=[SCALARS] + [VECTORS] * len(args),
        out_specs=[VECTORS] * len(outs),
        out_shape=list(outs),
        scratch_shapes=[pltpu.VMEM(shape, jnp.float32) for shape in scratch],
        compiler_params=pltpu.CompilerParams(vmem_limit_bytes=VMEM_LIMIT),
        cost_estimate=cost(flops),
        name=name,
    )(where, *args)


def swapped(block, axis, bit):
    count = lax.axis_size(axis)
    return lax.ppermute(block, axis, [(i, i ^ bit) for i in range(count)])


def gelu(values):
    return 0.5 * values * (1.0 + lax.erf(values * (0.5**0.5)))


def store_taps(hi_ref, lo_ref, act_ref, start):
    rows, channels = hi_ref.shape[0], act_ref.shape[1]
    for tap in range(KW):
        values = act_ref[pl.ds(start + tap, rows)]
        hi = values.astype(jnp.bfloat16)
        cols = slice(tap * channels, (tap + 1) * channels)
        hi_ref[:, cols] = hi
        lo_ref[:, cols] = (values - hi.astype(jnp.float32)).astype(jnp.bfloat16)


def row_plan(length, chunk):
    return chunk, length - chunk + 16, chunk // 2 - 4, (length - chunk) // 2 + 12


def padded(rows):
    return -(-rows // 16) * 16


def split_tap(where_ref, tap, w_ref, outs, far):
    channels, owned = w_ref.shape[0], w_ref.shape[1] // 4
    hi_ref, lo_ref = outs
    high = 1 - where_ref[0] if far else where_ref[0]
    core = where_ref[1]
    for half, owner in enumerate((2 * high + 1 - core, 2 * high + core)):
        weight = w_ref[:, pl.ds(pl.multiple_of(owner * owned, LANES), owned)]
        hi = weight.astype(jnp.bfloat16)
        place = (slice(tap * channels, (tap + 1) * channels), slice(half * owned, (half + 1) * owned))
        hi_ref[place] = hi
        lo_ref[place] = (weight - hi.astype(jnp.float32)).astype(jnp.bfloat16)


def opening_kernel(where_ref, gain_hbm, shift_hbm, x_hbm, w_hbm, hi_ref, lo_ref, edge_ref, far_hi, far_lo, own_hi, own_lo,
                   x_ref, gain_ref, shift_ref, act_ref, w_ref, x_sem, w_sem):
    length = x_ref.shape[1]
    gets = [
        pltpu.make_async_copy(src, dst, x_sem.at[i])
        for i, (src, dst) in enumerate(((gain_hbm, gain_ref), (shift_hbm, shift_ref), (x_hbm, x_ref)))
    ]
    copies = [pltpu.make_async_copy(w_hbm.at[tap], w_ref.at[tap], w_sem.at[tap]) for tap in range(KW)]
    for copy in gets + copies:
        copy.start()
    for copy in gets:
        copy.wait()
    gain, shift = gain_ref[...][None], shift_ref[...][None]
    rows = act_ref.shape[0]
    act_ref[...] = gelu(jnp.transpose(x_ref[:, :rows]) * gain + shift)
    edge_ref[0] = act_ref[:EDGE]
    last = jnp.transpose(x_ref[:, length - LANES :])[LANES - EDGE :]
    edge_ref[1] = gelu(last * gain + shift)
    store_taps(hi_ref, lo_ref, act_ref, 2)
    for tap, copy in enumerate(copies):
        copy.wait()
        split_tap(where_ref, tap, w_ref.at[tap], (far_hi, far_lo), True)
        split_tap(where_ref, tap, w_ref.at[tap], (own_hi, own_lo), False)


def opening(where, features, gain, shift, weight, rows):
    channels, length = features.shape
    outs = weight.shape[2]
    depth = KW * channels
    stack, split = bf16(padded(rows), depth), bf16(depth, outs // 2)
    span = -(-(padded(rows) + 6) // LANES) * LANES
    return pl.pallas_call(
        opening_kernel,
        in_specs=[SCALARS] + [IN_HBM] * 4,
        out_specs=[VECTORS] * 7,
        out_shape=[stack, stack, f32(2, EDGE, channels)] + [split] * 4,
        scratch_shapes=[
            pltpu.VMEM((channels, length), jnp.float32),
            pltpu.VMEM((channels,), jnp.float32),
            pltpu.VMEM((channels,), jnp.float32),
            pltpu.VMEM((span, channels), jnp.float32),
            pltpu.VMEM((KW, channels, outs), jnp.float32),
            pltpu.SemaphoreType.DMA((3,)),
            pltpu.SemaphoreType.DMA((KW,)),
        ],
        compiler_params=pltpu.CompilerParams(vmem_limit_bytes=16 * 1024 * 1024),
        cost_estimate=cost(LIGHT),
        name="opening",
    )(where, *map(in_hbm, (gain, shift, features, weight)))


def first_b_kernel(where_ref, x_ref, gain_ref, shift_ref, edge_ref, inner_ref, outer_ref, hi_ref, lo_ref, act_ref, *, chunk):
    gain, shift = gain_ref[...][None], shift_ref[...][None]
    length = x_ref.shape[1]
    base = (chunk + 2) // LANES * LANES
    top = length - base
    act_ref[:top] = gelu(jnp.transpose(x_ref[:, base:]) * gain + shift)
    odd = where_ref[5] > 0
    inner, outer = inner_ref[...], outer_ref[...]
    left = jnp.where(odd, inner, outer)
    right = jnp.where(odd, outer, inner)
    act_ref[top : top + 6] = right[:6]
    act_ref[top + 6 : top + 12] = left[2:]
    act_ref[top + 12 : top + 18] = edge_ref[0, :6]
    act_ref[top + 18 :] = jnp.zeros((act_ref.shape[0] - top - 18, act_ref.shape[1]), jnp.float32)
    store_taps(hi_ref, lo_ref, act_ref, chunk + 2 - base)


def split_kernel(where_ref, w_ref, hi_ref, lo_ref, *, far):
    for tap in range(KW):
        split_tap(where_ref, tap, w_ref.at[tap], (hi_ref, lo_ref), far)


def split_weight(where, weight, far):
    _, channels, outs = weight.shape
    return call(
        functools.partial(split_kernel, far=far), "split_far" if far else "split_own", where, [weight],
        [bf16(KW * channels, outs // 2)] * 2,
    )


def conv_kernel(where_ref, hi_ref, lo_ref, whi_ref, wlo_ref, there_ref, here_ref):
    rows, owned = there_ref.shape
    for start in range(0, 2 * owned, 2 * LANES):
        cols = slice(start, start + 2 * LANES)
        hi, weight_hi = hi_ref[...], whi_ref[:, cols]
        total = jnp.dot(hi, weight_hi, preferred_element_type=jnp.float32)
        total += jnp.dot(lo_ref[...], weight_hi, preferred_element_type=jnp.float32)
        total += jnp.dot(hi, wlo_ref[:, cols], preferred_element_type=jnp.float32)
        for part in range(2):
            at = start + part * LANES
            values = total[:rows, part * LANES : (part + 1) * LANES]
            if at < owned:
                there_ref[:, at : at + LANES] = values
            else:
                here_ref[:, at - owned : at - owned + LANES] = values


def conv(where, stack, weight, rows):
    owned = weight[0].shape[1] // 2
    depth = weight[0].shape[0]
    return call(
        conv_kernel, "conv", where, [*stack, *weight], [f32(rows, owned)] * 2
    )


def put_sum(sum_ref, start, a_ref, b_ref, c_ref):
    for j in range(sum_ref.shape[0]):
        cols = slice(j * LANES, (j + 1) * LANES)
        sum_ref[j, pl.ds(start, a_ref.shape[0])] = a_ref[:, cols] + (b_ref[:, cols] + c_ref[:, cols])


def pool_rows(sum_ref):
    blocks, rows, _ = sum_ref.shape
    return jnp.concatenate(
        [
            jnp.maximum(
                sum_ref[j, pl.ds(0, rows // 2, stride=2)], sum_ref[j, pl.ds(1, rows // 2, stride=2)]
            )
            for j in range(blocks)
        ],
        axis=1,
    )


def second_c_kernel(where_ref, a_ref, b_ref, c_ref, gain_ref, shift_ref, hi_ref, lo_ref, ends_ref, sum_ref, act_ref):
    put_sum(sum_ref, 0, a_ref, b_ref, c_ref)
    rows = a_ref.shape[0] // 2
    act_ref[:rows] = gelu(pool_rows(sum_ref) * gain_ref[...][None] + shift_ref[...][None])
    act_ref[rows:] = jnp.zeros((act_ref.shape[0] - rows, act_ref.shape[1]), jnp.float32)
    ends_ref[:4] = act_ref[:4]
    ends_ref[4:] = act_ref[rows - 4 : rows]
    store_taps(hi_ref, lo_ref, act_ref, 0)


def second_d_kernel(where_ref, a_ref, b_ref, c_ref, gain_ref, shift_ref, ends_ref, hi_ref, lo_ref, sum_ref, act_ref):
    put_sum(sum_ref, 0, a_ref, b_ref, c_ref)
    active = gelu(pool_rows(sum_ref) * gain_ref[...][None] + shift_ref[...][None])
    row = lax.broadcasted_iota(jnp.int32, active.shape, 0)
    main = active.shape[0] - 8
    beyond = (row >= main - 2) & (row < main) & (where_ref[3] == 0)
    before = (row >= main + 2) & (row < main + 4) & (where_ref[2] == 0)
    active = jnp.where(beyond | before, 0.0, active)
    act_ref[:4] = ends_ref[4:]
    act_ref[4 : main + 4] = active[:main]
    act_ref[main + 4 : main + 8] = active[main + 2 : main + 6]
    act_ref[main + 8 : main + 12] = ends_ref[:4]
    act_ref[main + 12 :] = jnp.zeros((act_ref.shape[0] - main - 12, act_ref.shape[1]), jnp.float32)
    store_taps(hi_ref, lo_ref, act_ref, 0)


def pieces_kernel(where_ref, *refs):
    ins, outs, (c_ref, d_ref, all_ref) = refs[:6], refs[6:-3], refs[-3:]
    put_sum(c_ref, 0, *ins[:3])
    put_sum(d_ref, 0, *ins[3:])
    pooled_d = pool_rows(d_ref)
    rows_c = ins[0].shape[0] // 2
    main = all_ref.shape[0] - 2 - rows_c
    all_ref[:2] = pooled_d[main + 2 : main + 4]
    all_ref[2 : 2 + rows_c] = pool_rows(c_ref)
    all_ref[2 + rows_c :] = pooled_d[:main]
    part = all_ref.shape[1] // GROUP
    turned = jnp.transpose(all_ref[...])
    member = where_ref[4]
    for r in range(GROUP):
        for d in range(GROUP):
            @pl.when(member == r ^ d)
            def _():
                outs[d][...] = turned[r * part : (r + 1) * part]


def join_kernel(where_ref, *refs):
    ins, out_ref = refs[:-1], refs[-1]
    width = ins[0].shape[1]
    for d, ref in enumerate(ins):
        out_ref[0, :, pl.ds(pl.multiple_of((where_ref[4] ^ d) * width, LANES), width)] = ref[...]


def after(values, *done):
    return lax.optimization_barrier((values, done))[0]


def body(features, gain_one, shift_one, wide_one, gain_two, shift_two, wide_two):
    seq = lax.axis_index("seq")
    n_seq = lax.axis_size("seq")
    ch = lax.axis_index("ch")
    where = jnp.stack(
        [
            ch // 2, ch % 2, (seq > 0).astype(jnp.int32), (seq < n_seq - 1).astype(jnp.int32),
            seq % GROUP, seq % 2,
        ]
    )
    one = [gain_one, shift_one]
    two = [gain_two, shift_two]
    channels, length = features.shape
    depth = KW * channels
    rows_a, rows_b, rows_c, rows_d = row_plan(length, CHUNK)

    hi_a, lo_a, edge, *split_one = opening(where, features, *one, wide_one, rows_a)
    far_one, own_one = split_one[:2], split_one[2:]
    odd = seq % 2
    to_inner = lax.dynamic_index_in_dim(edge, 1 - odd, 0, keepdims=False)
    to_outer = lax.dynamic_index_in_dim(edge, odd, 0, keepdims=False)
    inner = lax.ppermute(to_inner, "seq", [(i, i ^ 1) for i in range(n_seq)])
    outer = lax.ppermute(
        to_outer, "seq", [p for i in range(1, n_seq - 1, 2) for p in ((i, i + 1), (i + 1, i))]
    )

    there_a, here_a = conv(where, (hi_a, lo_a), far_one, rows_a)
    half_a = here_a + swapped(there_a, "ch", 1)
    sum_a = swapped(half_a, "ch", 2)

    stack_b = call(
        functools.partial(first_b_kernel, chunk=CHUNK), "first_b", where,
        [after(features, half_a), *one, edge, inner, outer],
        [bf16(padded(rows_b), depth)] * 2, [(length - (CHUNK + 2) // LANES * LANES + 48, channels)],
    )
    there_b, here_b = conv(where, stack_b, far_one, rows_b)
    half_b = here_b + swapped(there_b, "ch", 1)
    own_there_a, own_here_a = conv(where, after((hi_a, lo_a), there_b), own_one, rows_a)
    own_a = own_here_a, swapped(own_there_a, "ch", 1)
    half_b = after(half_b, own_here_a)
    sum_b = swapped(half_b, "ch", 2)

    own_there_b, own_here_b = conv(where, after(stack_b, half_b), own_one, rows_b)
    own_b = own_here_b, swapped(own_there_b, "ch", 1)
    far_two = split_weight(where, after(wide_two, own_here_b), True)

    *stack_c, ends = call(
        second_c_kernel, "second_c", where, [after(sum_a, far_two), *own_a, *two],
        [bf16(padded(rows_c), depth)] * 2 + [f32(8, channels)],
        [(channels // LANES, rows_a, LANES), (padded(rows_c) + 8, channels)],
    )
    there_c, here_c = conv(where, stack_c, far_two, rows_c)
    half_c = here_c + swapped(there_c, "ch", 1)
    own_two = split_weight(where, after(wide_two, there_c), False)
    half_c = after(half_c, own_two)
    sum_c = swapped(half_c, "ch", 2)

    stack_d = call(
        second_d_kernel, "second_d", where, [after(sum_b, half_c), *own_b, *two, ends],
        [bf16(padded(rows_d), depth)] * 2,
        [(channels // LANES, rows_b, LANES), (padded(rows_d) + 8, channels)],
    )
    there_d, here_d = conv(where, stack_d, far_two, rows_d)
    half_d = here_d + swapped(there_d, "ch", 1)
    own_there_c, own_here_c = conv(where, after(stack_c, there_d), own_two, rows_c)
    half_d = after(half_d, own_here_c)
    sum_d = swapped(half_d, "ch", 2)
    own_c = own_here_c, swapped(own_there_c, "ch", 1)
    own_there_d, own_here_d = conv(where, after(stack_d, half_d, sum_c), own_two, rows_d)
    own_d = own_here_d, swapped(own_there_d, "ch", 1)

    quarter = length // 4
    pieces = call(
        pieces_kernel, "pieces", where, [sum_c, *own_c, sum_d, *own_d],
        [f32(channels // GROUP, quarter)] * GROUP,
        [(channels // LANES, rows_c, LANES), (channels // LANES, rows_d, LANES), (quarter, channels)],
    )
    blocks = [pieces[0]] + [swapped(pieces[d], "seq", d) for d in range(1, GROUP)]
    shape = jax.ShapeDtypeStruct((1, channels // GROUP, GROUP * quarter), jnp.float32)
    return call(join_kernel, "join", where, blocks, [shape])[0]


def solution(mesh):
    return jax.shard_map(
        body,
        mesh=mesh,
        in_specs=(
            P("ch", "seq"),
            P("ch"),
            P("ch"),
            P(None, "ch", None),
            P("ch"),
            P("ch"),
            P(None, "ch", None),
        ),
        out_specs=P("seq", "ch", None),
        check_vma=False,
    )
```

```python
import functools

import jax
import jax.numpy as jnp
from jax import lax
from jax.experimental import pallas as pl
from jax.experimental.pallas import tpu as pltpu
from jax.sharding import PartitionSpec as P

KW = 5
GROUP = 4
EDGE = 8
CHUNK = 264
LANES = 128
VMEM_LIMIT = 2 * 1024 * 1024
VECTORS = pl.BlockSpec(memory_space=pltpu.VMEM)
IN_HBM = pl.BlockSpec(memory_space=pltpu.HBM)
LIGHT = 1_000_000_000
MIDDLE = 10 * LIGHT
EARLY = 30 * LIGHT
HEAVY = 300 * LIGHT


def f32(*shape):
    return jax.ShapeDtypeStruct(shape, jnp.float32)


def bf16(*shape):
    return jax.ShapeDtypeStruct(shape, jnp.bfloat16)


def in_hbm(array):
    return pltpu.with_memory_space_constraint(array, pltpu.HBM)


def cost(flops):
    return pl.CostEstimate(flops=flops, transcendentals=0, bytes_accessed=0)


def call(kernel, name, args, outs, scratch=(), flops=LIGHT):
    return pl.pallas_call(
        kernel,
        in_specs=[VECTORS] * len(args),
        out_specs=[VECTORS] * len(outs),
        out_shape=list(outs),
        scratch_shapes=[pltpu.VMEM(shape, jnp.float32) for shape in scratch],
        compiler_params=pltpu.CompilerParams(vmem_limit_bytes=VMEM_LIMIT),
        cost_estimate=cost(flops),
        name=name,
    )(*args)


def swapped(block, axis, bit):
    count = lax.axis_size(axis)
    return lax.ppermute(block, axis, [(i, i ^ bit) for i in range(count)])


def gelu(values):
    return 0.5 * values * (1.0 + lax.erf(values * (0.5**0.5)))


def store_taps(hi_ref, lo_ref, act_ref, start):
    rows, channels = hi_ref.shape[0], act_ref.shape[1]
    for tap in range(KW):
        values = act_ref[pl.ds(start + tap, rows)]
        hi = values.astype(jnp.bfloat16)
        cols = slice(tap * channels, (tap + 1) * channels)
        hi_ref[:, cols] = hi
        lo_ref[:, cols] = (values - hi.astype(jnp.float32)).astype(jnp.bfloat16)


def row_plan(length, chunk):
    return chunk, length - chunk + 16, chunk // 2 - 4, (length - chunk) // 2 + 12


def padded(rows):
    return -(-rows // 16) * 16


def split_tap(tap, w_ref, outs, far):
    channels, owned = w_ref.shape[0], w_ref.shape[1] // 4
    hi_ref, lo_ref = outs
    ch = lax.axis_index("ch")
    high, core = (1 - ch // 2 if far else ch // 2), ch % 2
    for half, owner in enumerate((2 * high + 1 - core, 2 * high + core)):
        weight = w_ref[:, pl.ds(pl.multiple_of(owner * owned, LANES), owned)]
        hi = weight.astype(jnp.bfloat16)
        place = (slice(tap * channels, (tap + 1) * channels), slice(half * owned, (half + 1) * owned))
        hi_ref[place] = hi
        lo_ref[place] = (weight - hi.astype(jnp.float32)).astype(jnp.bfloat16)


def opening_kernel(gain_hbm, shift_hbm, x_hbm, w_hbm, hi_ref, lo_ref, head_ref, inner_ref, outer_ref,
                   far_hi, far_lo, own_hi, own_lo,
                   x_ref, gain_ref, shift_ref, act_ref, w_ref, x_sem, w_sem):
    length = x_ref.shape[1]
    gets = [
        pltpu.make_async_copy(src, dst, x_sem.at[i])
        for i, (src, dst) in enumerate(((gain_hbm, gain_ref), (shift_hbm, shift_ref), (x_hbm, x_ref)))
    ]
    copies = [pltpu.make_async_copy(w_hbm.at[tap], w_ref.at[tap], w_sem.at[tap]) for tap in range(KW)]
    ahead = 2
    for copy in gets + copies[:ahead]:
        copy.start()
    for copy in gets:
        copy.wait()
    gain, shift = gain_ref[...][None], shift_ref[...][None]
    rows = act_ref.shape[0]
    act_ref[...] = gelu(jnp.transpose(x_ref[:, :rows]) * gain + shift)
    head = act_ref[:EDGE]
    tail = gelu(jnp.transpose(x_ref[:, length - LANES :])[LANES - EDGE :] * gain + shift)
    odd = lax.axis_index("seq") % 2 == 1
    head_ref[...] = head
    inner_ref[...] = jnp.where(odd, head, tail)
    outer_ref[...] = jnp.where(odd, tail, head)
    store_taps(hi_ref, lo_ref, act_ref, 2)
    for tap, copy in enumerate(copies):
        copy.wait()
        if tap + ahead < KW:
            copies[tap + ahead].start()
        split_tap(tap, w_ref.at[tap], (far_hi, far_lo), True)
        split_tap(tap, w_ref.at[tap], (own_hi, own_lo), False)


def opening(features, gain, shift, weight, rows):
    channels, length = features.shape
    outs = weight.shape[2]
    depth = KW * channels
    stack, split = bf16(padded(rows), depth), bf16(depth, outs // 2)
    span = -(-(padded(rows) + 6) // LANES) * LANES
    return pl.pallas_call(
        opening_kernel,
        in_specs=[IN_HBM] * 4,
        out_specs=[VECTORS] * 9,
        out_shape=[stack] * 2 + [f32(EDGE, channels)] * 3 + [split] * 4,
        scratch_shapes=[
            pltpu.VMEM((channels, length), jnp.float32),
            pltpu.VMEM((channels,), jnp.float32),
            pltpu.VMEM((channels,), jnp.float32),
            pltpu.VMEM((span, channels), jnp.float32),
            pltpu.VMEM((KW, channels, outs), jnp.float32),
            pltpu.SemaphoreType.DMA((3,)),
            pltpu.SemaphoreType.DMA((KW,)),
        ],
        compiler_params=pltpu.CompilerParams(vmem_limit_bytes=16 * 1024 * 1024),
        cost_estimate=cost(LIGHT),
        name="opening",
    )(*map(in_hbm, (gain, shift, features, weight)))


def first_b_kernel(x_ref, gain_ref, shift_ref, head_ref, inner_ref, outer_ref, hi_ref, lo_ref, act_ref, *, chunk):
    gain, shift = gain_ref[...][None], shift_ref[...][None]
    length = x_ref.shape[1]
    base = (chunk + 2) // LANES * LANES
    top = length - base
    act_ref[:top] = gelu(jnp.transpose(x_ref[:, base:]) * gain + shift)
    odd = lax.axis_index("seq") % 2 == 1
    inner, outer = inner_ref[...], outer_ref[...]
    left = jnp.where(odd, inner, outer)
    right = jnp.where(odd, outer, inner)
    act_ref[top : top + 6] = right[:6]
    act_ref[top + 6 : top + 12] = left[2:]
    act_ref[top + 12 : top + 18] = head_ref[:6]
    act_ref[top + 18 :] = jnp.zeros((act_ref.shape[0] - top - 18, act_ref.shape[1]), jnp.float32)
    store_taps(hi_ref, lo_ref, act_ref, chunk + 2 - base)


def split_kernel(w_ref, hi_ref, lo_ref, *, far):
    for tap in range(KW):
        split_tap(tap, w_ref.at[tap], (hi_ref, lo_ref), far)


def split_weight(weight, far, flops=LIGHT):
    _, channels, outs = weight.shape
    return call(
        functools.partial(split_kernel, far=far), "split_far" if far else "split_own", [weight],
        [bf16(KW * channels, outs // 2)] * 2, flops=flops,
    )


def conv_kernel(hi_ref, lo_ref, whi_ref, wlo_ref, there_ref, here_ref):
    rows, owned = there_ref.shape
    for start in range(0, 2 * owned, 2 * LANES):
        cols = slice(start, start + 2 * LANES)
        hi, weight_hi = hi_ref[...], whi_ref[:, cols]
        total = jnp.dot(hi, weight_hi, preferred_element_type=jnp.float32)
        total += jnp.dot(lo_ref[...], weight_hi, preferred_element_type=jnp.float32)
        total += jnp.dot(hi, wlo_ref[:, cols], preferred_element_type=jnp.float32)
        for part in range(2):
            at = start + part * LANES
            values = total[:rows, part * LANES : (part + 1) * LANES]
            if at < owned:
                there_ref[:, at : at + LANES] = values
            else:
                here_ref[:, at - owned : at - owned + LANES] = values


def conv(stack, weight, rows, flops=LIGHT):
    owned = weight[0].shape[1] // 2
    depth = weight[0].shape[0]
    return call(
        conv_kernel, "conv", [*stack, *weight], [f32(rows, owned)] * 2, flops=flops
    )


def add_kernel(a_ref, b_ref, out_ref):
    out_ref[...] = a_ref[...] + b_ref[...]


def added(a, b):
    return call(add_kernel, "added", [a, b], [f32(*a.shape)])[0]


def put_sum(sum_ref, *refs):
    for j in range(sum_ref.shape[0]):
        cols = slice(j * LANES, (j + 1) * LANES)
        sum_ref[j] = sum(ref[:, cols] for ref in refs)


def pool_rows(sum_ref):
    blocks, rows, _ = sum_ref.shape
    return jnp.concatenate(
        [
            jnp.maximum(
                sum_ref[j, pl.ds(0, rows // 2, stride=2)], sum_ref[j, pl.ds(1, rows // 2, stride=2)]
            )
            for j in range(blocks)
        ],
        axis=1,
    )


def second_c_kernel(a_ref, b_ref, c_ref, gain_ref, shift_ref, hi_ref, lo_ref, ends_ref, sum_ref, act_ref):
    put_sum(sum_ref, a_ref, b_ref, c_ref)
    rows = a_ref.shape[0] // 2
    act_ref[:rows] = gelu(pool_rows(sum_ref) * gain_ref[...][None] + shift_ref[...][None])
    act_ref[rows:] = jnp.zeros((act_ref.shape[0] - rows, act_ref.shape[1]), jnp.float32)
    ends_ref[:4] = act_ref[:4]
    ends_ref[4:] = act_ref[rows - 4 : rows]
    store_taps(hi_ref, lo_ref, act_ref, 0)


def second_d_kernel(a_ref, b_ref, c_ref, gain_ref, shift_ref, ends_ref, hi_ref, lo_ref, sum_ref, act_ref):
    put_sum(sum_ref, a_ref, b_ref, c_ref)
    active = gelu(pool_rows(sum_ref) * gain_ref[...][None] + shift_ref[...][None])
    row = lax.broadcasted_iota(jnp.int32, active.shape, 0)
    main = active.shape[0] - 8
    seq = lax.axis_index("seq")
    ends = lax.axis_size("seq") - 1
    beyond = (row >= main - 2) & (row < main) & (seq == ends)
    before = (row >= main + 2) & (row < main + 4) & (seq == 0)
    active = jnp.where(beyond | before, 0.0, active)
    act_ref[:4] = ends_ref[4:]
    act_ref[4 : main + 4] = active[:main]
    act_ref[main + 4 : main + 8] = active[main + 2 : main + 6]
    act_ref[main + 8 : main + 12] = ends_ref[:4]
    act_ref[main + 12 :] = jnp.zeros((act_ref.shape[0] - main - 12, act_ref.shape[1]), jnp.float32)
    store_taps(hi_ref, lo_ref, act_ref, 0)


def pieces_kernel(*refs):
    ins, outs, (c_ref, d_ref, all_ref) = refs[:5], refs[5:-3], refs[-3:]
    put_sum(c_ref, *ins[:3])
    put_sum(d_ref, *ins[3:])
    pooled_d = pool_rows(d_ref)
    rows_c = ins[0].shape[0] // 2
    main = all_ref.shape[0] - 2 - rows_c
    all_ref[:2] = pooled_d[main + 2 : main + 4]
    all_ref[2 : 2 + rows_c] = pool_rows(c_ref)
    all_ref[2 + rows_c :] = pooled_d[:main]
    part = all_ref.shape[1] // GROUP
    turned = jnp.transpose(all_ref[...])
    member = lax.axis_index("seq") % GROUP
    for r in range(GROUP):
        for d in range(GROUP):
            @pl.when(member == r ^ d)
            def _():
                outs[d][...] = turned[r * part : (r + 1) * part]


def join_kernel(*refs):
    ins, out_ref = refs[:-1], refs[-1]
    width = ins[0].shape[1]
    member = lax.axis_index("seq") % GROUP
    for d, ref in enumerate(ins):
        out_ref[0, :, pl.ds(pl.multiple_of((member ^ d) * width, LANES), width)] = ref[...]


def after(values, *done):
    return lax.optimization_barrier((values, done))[0]


def body(features, gain_one, shift_one, wide_one, gain_two, shift_two, wide_two):
    n_seq = lax.axis_size("seq")
    one = [gain_one, shift_one]
    two = [gain_two, shift_two]
    channels, length = features.shape
    depth = KW * channels
    rows_a, rows_b, rows_c, rows_d = row_plan(length, CHUNK)

    hi_a, lo_a, head, to_inner, to_outer, *split_one = opening(features, *one, wide_one, rows_a)
    far_one, own_one = split_one[:2], split_one[2:]
    there_a, here_a = conv((hi_a, lo_a), far_one, rows_a)
    half_a = added(here_a, swapped(there_a, "ch", 1))
    sum_a = swapped(half_a, "ch", 2)

    to_inner, to_outer = after((to_inner, to_outer), half_a)
    inner = lax.ppermute(to_inner, "seq", [(i, i ^ 1) for i in range(n_seq)])
    outer = lax.ppermute(
        to_outer, "seq", [p for i in range(1, n_seq - 1, 2) for p in ((i, i + 1), (i + 1, i))]
    )
    own_there_a, own_here_a = conv(after((hi_a, lo_a), half_a), own_one, rows_a, EARLY)
    own_a = own_here_a, swapped(own_there_a, "ch", 1)
    stack_b = call(
        functools.partial(first_b_kernel, chunk=CHUNK), "first_b",
        [after(features, own_here_a), *one, head, inner, outer],
        [bf16(padded(rows_b), depth)] * 2, [(length - (CHUNK + 2) // LANES * LANES + 48, channels)], EARLY,
    )
    there_b, here_b = conv(stack_b, far_one, rows_b, EARLY)
    half_b = added(here_b, swapped(there_b, "ch", 1))
    far_two = split_weight(after(wide_two, there_b), True, EARLY)
    half_b = after(half_b, far_two)
    sum_b = swapped(half_b, "ch", 2)

    own_there_b, own_here_b = conv(after(stack_b, half_b), own_one, rows_b)
    own_b = own_here_b, swapped(own_there_b, "ch", 1)

    *stack_c, ends = call(
        second_c_kernel, "second_c", [after(sum_a, own_here_b), *own_a, *two],
        [bf16(padded(rows_c), depth)] * 2 + [f32(8, channels)],
        [(channels // LANES, rows_a, LANES), (padded(rows_c) + 8, channels)],
    )
    there_c, here_c = conv(stack_c, far_two, rows_c)
    own_two = split_weight(after(wide_two, there_c), False)
    half_c = added(here_c, swapped(there_c, "ch", 1))
    half_c = after(half_c, own_two)
    sum_c = swapped(half_c, "ch", 2)

    stack_d = call(
        second_d_kernel, "second_d", [after(sum_b, half_c), *own_b, *two, ends],
        [bf16(padded(rows_d), depth)] * 2,
        [(channels // LANES, rows_b, LANES), (padded(rows_d) + 8, channels)], MIDDLE,
    )
    there_d, here_d = conv(stack_d, far_two, rows_d, MIDDLE)
    half_d = added(here_d, swapped(there_d, "ch", 1))
    own_there_c, own_here_c = conv(after(stack_c, there_d), own_two, rows_c, MIDDLE)
    half_d = after(half_d, own_here_c)
    sum_d = swapped(half_d, "ch", 2)
    own_there_d, own_here_d = conv(after(stack_d, half_d, sum_c), own_two, rows_d)
    here_d = call(add_kernel, "added", [sum_d, own_here_d], [f32(*sum_d.shape)], flops=HEAVY)[0]
    last_c, last_d = after((swapped(own_there_c, "ch", 1), swapped(own_there_d, "ch", 1)), here_d)

    quarter = length // 4
    pieces = call(
        pieces_kernel, "pieces", [sum_c, own_here_c, last_c, here_d, last_d],
        [f32(channels // GROUP, quarter)] * GROUP,
        [(channels // LANES, rows_c, LANES), (channels // LANES, rows_d, LANES), (quarter, channels)],
    )
    blocks = [pieces[0]] + [swapped(pieces[d], "seq", d) for d in range(1, GROUP)]
    shape = jax.ShapeDtypeStruct((1, channels // GROUP, GROUP * quarter), jnp.float32)
    return call(join_kernel, "join", blocks, [shape])[0]


def solution(mesh):
    return jax.shard_map(
        body,
        mesh=mesh,
        in_specs=(
            P("ch", "seq"),
            P("ch"),
            P("ch"),
            P(None, "ch", None),
            P("ch"),
            P("ch"),
            P(None, "ch", None),
        ),
        out_specs=P("seq", "ch", None),
        check_vma=False,
    )
```

```python
import functools

import jax
import jax.numpy as jnp
from jax import lax
from jax.experimental import pallas as pl
from jax.experimental.pallas import tpu as pltpu
from jax.sharding import PartitionSpec as P

KW = 5
GROUP = 4
EDGE = 8
CHUNK = 296
LANES = 128
VMEM_LIMIT = 2 * 1024 * 1024
VECTORS = pl.BlockSpec(memory_space=pltpu.VMEM)
IN_HBM = pl.BlockSpec(memory_space=pltpu.HBM)
LIGHT = 1_000_000_000
MIDDLE = 10 * LIGHT
EARLY = 30 * LIGHT
HEAVY = 300 * LIGHT


def f32(*shape):
    return jax.ShapeDtypeStruct(shape, jnp.float32)


def bf16(*shape):
    return jax.ShapeDtypeStruct(shape, jnp.bfloat16)


def in_hbm(array):
    return pltpu.with_memory_space_constraint(array, pltpu.HBM)


def cost(flops):
    return pl.CostEstimate(flops=flops, transcendentals=0, bytes_accessed=0)


def call(kernel, name, args, outs, scratch=(), flops=LIGHT):
    return pl.pallas_call(
        kernel,
        in_specs=[VECTORS] * len(args),
        out_specs=[VECTORS] * len(outs),
        out_shape=list(outs),
        scratch_shapes=[pltpu.VMEM(shape, jnp.float32) for shape in scratch],
        compiler_params=pltpu.CompilerParams(vmem_limit_bytes=VMEM_LIMIT),
        cost_estimate=cost(flops),
        name=name,
    )(*args)


def swapped(block, axis, bit):
    count = lax.axis_size(axis)
    return lax.ppermute(block, axis, [(i, i ^ bit) for i in range(count)])


def gelu(values):
    return 0.5 * values * (1.0 + lax.erf(values * (0.5**0.5)))


def store_taps(hi_ref, lo_ref, act_ref, start):
    rows, channels = hi_ref.shape[0], act_ref.shape[1]
    for tap in range(KW):
        values = act_ref[pl.ds(start + tap, rows)]
        hi = values.astype(jnp.bfloat16)
        cols = slice(tap * channels, (tap + 1) * channels)
        hi_ref[:, cols] = hi
        lo_ref[:, cols] = (values - hi.astype(jnp.float32)).astype(jnp.bfloat16)


def row_plan(length, chunk):
    return chunk, length - chunk + 16, chunk // 2 - 4, (length - chunk) // 2 + 12


def padded(rows):
    return -(-rows // 16) * 16


def half_columns(outs, far):
    high = lax.axis_index("ch") // 2
    return pl.ds(pl.multiple_of((1 - high if far else high) * (outs // 2), LANES), outs // 2)


def split_tap(tap, w_ref, hi_ref, lo_ref):
    channels, owned = w_ref.shape[0], w_ref.shape[1] // 2
    core = lax.axis_index("ch") % 2
    for half, owner in enumerate((1 - core, core)):
        weight = w_ref[:, pl.ds(pl.multiple_of(owner * owned, LANES), owned)]
        hi = weight.astype(jnp.bfloat16)
        place = (slice(tap * channels, (tap + 1) * channels), slice(half * owned, (half + 1) * owned))
        hi_ref[place] = hi
        lo_ref[place] = (weight - hi.astype(jnp.float32)).astype(jnp.bfloat16)


def opening_kernel(gain_hbm, shift_hbm, x_hbm, w_hbm, hi_ref, lo_ref, head_ref, inner_ref, outer_ref, far_hi, far_lo,
                                      x_ref, gain_ref, shift_ref, act_ref, w_ref, x_sem, w_sem):
    length = x_ref.shape[1]
    gets = [
        pltpu.make_async_copy(src, dst, x_sem.at[i])
        for i, (src, dst) in enumerate(((gain_hbm, gain_ref), (shift_hbm, shift_ref), (x_hbm, x_ref)))
    ]
    cols = half_columns(w_hbm.shape[2], True)
    copies = [
        pltpu.make_async_copy(w_hbm.at[tap, :, cols], w_ref.at[tap], w_sem.at[tap]) for tap in range(KW)
    ]
    ahead = KW
    for copy in gets + copies[:ahead]:
        copy.start()
    for copy in gets:
        copy.wait()
    gain, shift = gain_ref[...][None], shift_ref[...][None]
    rows = act_ref.shape[0]
    act_ref[...] = gelu(jnp.transpose(x_ref[:, :rows]) * gain + shift)
    head = act_ref[:EDGE]
    tail = gelu(jnp.transpose(x_ref[:, length - LANES :])[LANES - EDGE :] * gain + shift)
    odd = lax.axis_index("seq") % 2 == 1
    head_ref[...] = head
    inner_ref[...] = jnp.where(odd, head, tail)
    outer_ref[...] = jnp.where(odd, tail, head)
    store_taps(hi_ref, lo_ref, act_ref, 2)
    for tap, copy in enumerate(copies):
        copy.wait()
        if tap + ahead < KW:
            copies[tap + ahead].start()
        split_tap(tap, w_ref.at[tap], far_hi, far_lo)


def opening(features, gain, shift, weight, rows):
    channels, length = features.shape
    outs = weight.shape[2]
    depth = KW * channels
    stack, split = bf16(padded(rows), depth), bf16(depth, outs // 2)
    span = -(-(padded(rows) + 6) // LANES) * LANES
    return pl.pallas_call(
        opening_kernel,
        in_specs=[IN_HBM] * 4,
        out_specs=[VECTORS] * 7,
        out_shape=[stack] * 2 + [f32(EDGE, channels)] * 3 + [split] * 2,
        scratch_shapes=[
            pltpu.VMEM((channels, length), jnp.float32),
            pltpu.VMEM((channels,), jnp.float32),
            pltpu.VMEM((channels,), jnp.float32),
            pltpu.VMEM((span, channels), jnp.float32),
            pltpu.VMEM((KW, channels, outs // 2), jnp.float32),
            pltpu.SemaphoreType.DMA((3,)),
            pltpu.SemaphoreType.DMA((KW,)),
        ],
        compiler_params=pltpu.CompilerParams(vmem_limit_bytes=10 * 1024 * 1024),
        cost_estimate=cost(LIGHT),
        name="opening",
    )(*map(in_hbm, (gain, shift, features, weight)))


def first_b_kernel(x_ref, gain_ref, shift_ref, head_ref, inner_ref, outer_ref, hi_ref, lo_ref, act_ref, *, chunk):
    gain, shift = gain_ref[...][None], shift_ref[...][None]
    length = x_ref.shape[1]
    base = (chunk + 2) // LANES * LANES
    top = length - base
    act_ref[:top] = gelu(jnp.transpose(x_ref[:, base:]) * gain + shift)
    odd = lax.axis_index("seq") % 2 == 1
    inner, outer = inner_ref[...], outer_ref[...]
    left = jnp.where(odd, inner, outer)
    right = jnp.where(odd, outer, inner)
    act_ref[top : top + 6] = right[:6]
    act_ref[top + 6 : top + 12] = left[2:]
    act_ref[top + 12 : top + 18] = head_ref[:6]
    act_ref[top + 18 :] = jnp.zeros((act_ref.shape[0] - top - 18, act_ref.shape[1]), jnp.float32)
    store_taps(hi_ref, lo_ref, act_ref, chunk + 2 - base)


def split_kernel(w_ref, hi_ref, lo_ref, *, far):
    outs = 2 * hi_ref.shape[1]
    for tap in range(KW):
        block = w_ref.at[tap]
        if w_ref.shape[2] == outs:
            block = block.at[:, half_columns(outs, far)]
        split_tap(tap, block, hi_ref, lo_ref)


def split_weight(weight, outs, far, flops=LIGHT):
    _, channels, _ = weight.shape
    return call(
        functools.partial(split_kernel, far=far), "split_far" if far else "split_own", [weight],
        [bf16(KW * channels, outs // 2)] * 2, flops=flops,
    )


def conv_kernel(hi_ref, lo_ref, whi_ref, wlo_ref, there_ref, here_ref):
    rows, owned = there_ref.shape
    for start in range(0, 2 * owned, 2 * LANES):
        cols = slice(start, start + 2 * LANES)
        hi, weight_hi = hi_ref[...], whi_ref[:, cols]
        total = jnp.dot(hi, weight_hi, preferred_element_type=jnp.float32)
        total += jnp.dot(lo_ref[...], weight_hi, preferred_element_type=jnp.float32)
        total += jnp.dot(hi, wlo_ref[:, cols], preferred_element_type=jnp.float32)
        for part in range(2):
            at = start + part * LANES
            values = total[:rows, part * LANES : (part + 1) * LANES]
            if at < owned:
                there_ref[:, at : at + LANES] = values
            else:
                here_ref[:, at - owned : at - owned + LANES] = values


def conv(stack, weight, rows, flops=LIGHT):
    owned = weight[0].shape[1] // 2
    depth = weight[0].shape[0]
    return call(
        conv_kernel, "conv", [*stack, *weight], [f32(rows, owned)] * 2, flops=flops
    )


def add_kernel(a_ref, b_ref, out_ref):
    out_ref[...] = a_ref[...] + b_ref[...]


def added(a, b):
    return call(add_kernel, "added", [a, b], [f32(*a.shape)])[0]


def put_sum(sum_ref, *refs):
    for j in range(sum_ref.shape[0]):
        cols = slice(j * LANES, (j + 1) * LANES)
        sum_ref[j] = sum(ref[:, cols] for ref in refs)


def pool_rows(sum_ref):
    blocks, rows, _ = sum_ref.shape
    return jnp.concatenate(
        [
            jnp.maximum(
                sum_ref[j, pl.ds(0, rows // 2, stride=2)], sum_ref[j, pl.ds(1, rows // 2, stride=2)]
            )
            for j in range(blocks)
        ],
        axis=1,
    )


def second_c_kernel(a_ref, b_ref, c_ref, gain_ref, shift_ref, hi_ref, lo_ref, ends_ref, sum_ref, act_ref):
    put_sum(sum_ref, a_ref, b_ref, c_ref)
    rows = a_ref.shape[0] // 2
    act_ref[:rows] = gelu(pool_rows(sum_ref) * gain_ref[...][None] + shift_ref[...][None])
    act_ref[rows:] = jnp.zeros((act_ref.shape[0] - rows, act_ref.shape[1]), jnp.float32)
    ends_ref[:4] = act_ref[:4]
    ends_ref[4:] = act_ref[rows - 4 : rows]
    store_taps(hi_ref, lo_ref, act_ref, 0)


def second_d_kernel(a_ref, b_ref, c_ref, gain_ref, shift_ref, ends_ref, hi_ref, lo_ref, sum_ref, act_ref):
    put_sum(sum_ref, a_ref, b_ref, c_ref)
    active = gelu(pool_rows(sum_ref) * gain_ref[...][None] + shift_ref[...][None])
    row = lax.broadcasted_iota(jnp.int32, active.shape, 0)
    main = active.shape[0] - 8
    seq = lax.axis_index("seq")
    ends = lax.axis_size("seq") - 1
    beyond = (row >= main - 2) & (row < main) & (seq == ends)
    before = (row >= main + 2) & (row < main + 4) & (seq == 0)
    active = jnp.where(beyond | before, 0.0, active)
    act_ref[:4] = ends_ref[4:]
    act_ref[4 : main + 4] = active[:main]
    act_ref[main + 4 : main + 8] = active[main + 2 : main + 6]
    act_ref[main + 8 : main + 12] = ends_ref[:4]
    act_ref[main + 12 :] = jnp.zeros((act_ref.shape[0] - main - 12, act_ref.shape[1]), jnp.float32)
    store_taps(hi_ref, lo_ref, act_ref, 0)


def pieces_kernel(*refs):
    ins, outs, (c_ref, d_ref, all_ref) = refs[:5], refs[5:-3], refs[-3:]
    put_sum(c_ref, *ins[:3])
    put_sum(d_ref, *ins[3:])
    pooled_d = pool_rows(d_ref)
    rows_c = ins[0].shape[0] // 2
    main = all_ref.shape[0] - 2 - rows_c
    all_ref[:2] = pooled_d[main + 2 : main + 4]
    all_ref[2 : 2 + rows_c] = pool_rows(c_ref)
    all_ref[2 + rows_c :] = pooled_d[:main]
    part = all_ref.shape[1] // GROUP
    turned = jnp.transpose(all_ref[...])
    member = lax.axis_index("seq") % GROUP
    for r in range(GROUP):
        for d in range(GROUP):
            @pl.when(member == r ^ d)
            def _():
                outs[d][...] = turned[r * part : (r + 1) * part]


def join_kernel(*refs):
    ins, out_ref = refs[:-1], refs[-1]
    width = ins[0].shape[1]
    member = lax.axis_index("seq") % GROUP
    for d, ref in enumerate(ins):
        out_ref[0, :, pl.ds(pl.multiple_of((member ^ d) * width, LANES), width)] = ref[...]


def after(values, *done):
    return lax.optimization_barrier((values, done))[0]


def body(features, gain_one, shift_one, wide_one, gain_two, shift_two, wide_two):
    n_seq = lax.axis_size("seq")
    one = [gain_one, shift_one]
    two = [gain_two, shift_two]
    channels, length = features.shape
    depth = KW * channels
    rows_a, rows_b, rows_c, rows_d = row_plan(length, CHUNK)

    outs = wide_one.shape[2]

    hi_a, lo_a, head, to_inner, to_outer, *far_one = opening(features, *one, wide_one, rows_a)
    there_a, here_a = conv((hi_a, lo_a), far_one, rows_a)
    own_one = split_weight(after(wide_one, there_a), outs, False)
    half_a = after(added(here_a, swapped(there_a, "ch", 1)), own_one)
    sum_a = swapped(half_a, "ch", 2)

    to_inner, to_outer = after((to_inner, to_outer), half_a)
    inner = lax.ppermute(to_inner, "seq", [(i, i ^ 1) for i in range(n_seq)])
    outer = lax.ppermute(
        to_outer, "seq", [p for i in range(1, n_seq - 1, 2) for p in ((i, i + 1), (i + 1, i))]
    )
    own_there_a, own_here_a = conv(after((hi_a, lo_a), half_a), own_one, rows_a, EARLY)
    own_a = own_here_a, swapped(own_there_a, "ch", 1)
    stack_b = call(
        functools.partial(first_b_kernel, chunk=CHUNK), "first_b",
        [after(features, own_here_a), *one, head, inner, outer],
        [bf16(padded(rows_b), depth)] * 2, [(length - (CHUNK + 2) // LANES * LANES + 48, channels)], EARLY,
    )
    there_b, here_b = conv(stack_b, far_one, rows_b, EARLY)
    half_b = added(here_b, swapped(there_b, "ch", 1))
    far_two = split_weight(after(wide_two, there_b), outs, True, EARLY)
    half_b = after(half_b, far_two)
    sum_b = swapped(half_b, "ch", 2)

    own_there_b, own_here_b = conv(after(stack_b, half_b), own_one, rows_b)
    own_b = own_here_b, swapped(own_there_b, "ch", 1)

    *stack_c, ends = call(
        second_c_kernel, "second_c", [after(sum_a, own_here_b), *own_a, *two],
        [bf16(padded(rows_c), depth)] * 2 + [f32(8, channels)],
        [(channels // LANES, rows_a, LANES), (padded(rows_c) + 8, channels)],
    )
    there_c, here_c = conv(stack_c, far_two, rows_c)
    own_two = split_weight(after(wide_two, there_c), outs, False)
    half_c = added(here_c, swapped(there_c, "ch", 1))
    half_c = after(half_c, own_two)
    sum_c = swapped(half_c, "ch", 2)

    stack_d = call(
        second_d_kernel, "second_d", [after(sum_b, half_c), *own_b, *two, ends],
        [bf16(padded(rows_d), depth)] * 2,
        [(channels // LANES, rows_b, LANES), (padded(rows_d) + 8, channels)], MIDDLE,
    )
    there_d, here_d = conv(stack_d, far_two, rows_d, MIDDLE)
    half_d = added(here_d, swapped(there_d, "ch", 1))
    own_there_c, own_here_c = conv(after(stack_c, there_d), own_two, rows_c, MIDDLE)
    half_d = after(half_d, own_here_c)
    sum_d = swapped(half_d, "ch", 2)
    own_there_d, own_here_d = conv(after(stack_d, half_d, sum_c), own_two, rows_d)
    here_d = call(add_kernel, "added", [sum_d, own_here_d], [f32(*sum_d.shape)], flops=HEAVY)[0]
    last_c, last_d = after((swapped(own_there_c, "ch", 1), swapped(own_there_d, "ch", 1)), here_d)

    quarter = length // 4
    pieces = call(
        pieces_kernel, "pieces", [sum_c, own_here_c, last_c, here_d, last_d],
        [f32(channels // GROUP, quarter)] * GROUP,
        [(channels // LANES, rows_c, LANES), (channels // LANES, rows_d, LANES), (quarter, channels)],
    )
    blocks = [pieces[0]] + [swapped(pieces[d], "seq", d) for d in range(1, GROUP)]
    shape = jax.ShapeDtypeStruct((1, channels // GROUP, GROUP * quarter), jnp.float32)
    return call(join_kernel, "join", blocks, [shape])[0]


def solution(mesh):
    return jax.shard_map(
        body,
        mesh=mesh,
        in_specs=(
            P("ch", "seq"),
            P("ch"),
            P("ch"),
            P(None, "ch", None),
            P("ch"),
            P("ch"),
            P(None, "ch", None),
        ),
        out_specs=P("seq", "ch", None),
        check_vma=False,
    )
```

```python
import functools

import jax
import jax.numpy as jnp
from jax import lax
from jax.experimental import pallas as pl
from jax.experimental.pallas import tpu as pltpu
from jax.sharding import PartitionSpec as P

KW = 5
GROUP = 4
EDGE = 8
CHUNK = 296
LANES = 128
VMEM_LIMIT = 2 * 1024 * 1024
VECTORS = pl.BlockSpec(memory_space=pltpu.VMEM)
IN_HBM = pl.BlockSpec(memory_space=pltpu.HBM)
LIGHT = 1_000_000_000
MIDDLE = 10 * LIGHT
EARLY = 30 * LIGHT
HEAVY = 30 * LIGHT


def f32(*shape):
    return jax.ShapeDtypeStruct(shape, jnp.float32)


def bf16(*shape):
    return jax.ShapeDtypeStruct(shape, jnp.bfloat16)


def in_hbm(array):
    return pltpu.with_memory_space_constraint(array, pltpu.HBM)


def cost(flops):
    return pl.CostEstimate(flops=flops, transcendentals=0, bytes_accessed=0)


def call(kernel, name, args, outs, scratch=(), flops=LIGHT):
    return pl.pallas_call(
        kernel,
        in_specs=[VECTORS] * len(args),
        out_specs=[VECTORS] * len(outs),
        out_shape=list(outs),
        scratch_shapes=[pltpu.VMEM(shape, jnp.float32) for shape in scratch],
        compiler_params=pltpu.CompilerParams(vmem_limit_bytes=VMEM_LIMIT),
        cost_estimate=cost(flops),
        name=name,
    )(*args)


def swapped(block, axis, bit):
    count = lax.axis_size(axis)
    return lax.ppermute(block, axis, [(i, i ^ bit) for i in range(count)])


def gelu(values):
    return 0.5 * values * (1.0 + lax.erf(values * (0.5**0.5)))


def store_taps(hi_ref, lo_ref, act_ref, start):
    rows, channels = hi_ref.shape[0], act_ref.shape[1]
    for tap in range(KW):
        values = act_ref[pl.ds(start + tap, rows)]
        hi = values.astype(jnp.bfloat16)
        cols = slice(tap * channels, (tap + 1) * channels)
        hi_ref[:, cols] = hi
        lo_ref[:, cols] = (values - hi.astype(jnp.float32)).astype(jnp.bfloat16)


def row_plan(length, chunk):
    return chunk, length - chunk + 16, chunk // 2 - 4, (length - chunk) // 2 + 12


def padded(rows):
    return -(-rows // 16) * 16


def half_columns(outs, far):
    high = lax.axis_index("ch") // 2
    return pl.ds(pl.multiple_of((1 - high if far else high) * (outs // 2), LANES), outs // 2)


def split_tap(tap, w_ref, hi_ref, lo_ref):
    channels, owned = w_ref.shape[0], w_ref.shape[1] // 2
    core = lax.axis_index("ch") % 2
    for half, owner in enumerate((1 - core, core)):
        weight = w_ref[:, pl.ds(pl.multiple_of(owner * owned, LANES), owned)]
        hi = weight.astype(jnp.bfloat16)
        place = (slice(tap * channels, (tap + 1) * channels), slice(half * owned, (half + 1) * owned))
        hi_ref[place] = hi
        lo_ref[place] = (weight - hi.astype(jnp.float32)).astype(jnp.bfloat16)


def opening_kernel(gain_hbm, shift_hbm, x_hbm, w_hbm, hi_ref, lo_ref, head_ref, inner_ref, outer_ref, far_hi, far_lo,
                                      x_ref, gain_ref, shift_ref, act_ref, w_ref, x_sem, w_sem):
    length = x_ref.shape[1]
    gets = [
        pltpu.make_async_copy(src, dst, x_sem.at[i])
        for i, (src, dst) in enumerate(((gain_hbm, gain_ref), (shift_hbm, shift_ref), (x_hbm, x_ref)))
    ]
    cols = half_columns(w_hbm.shape[2], True)
    copies = [
        pltpu.make_async_copy(w_hbm.at[tap, :, cols], w_ref.at[tap], w_sem.at[tap]) for tap in range(KW)
    ]
    ahead = KW
    for copy in gets + copies[:ahead]:
        copy.start()
    for copy in gets:
        copy.wait()
    gain, shift = gain_ref[...][None], shift_ref[...][None]
    rows = act_ref.shape[0]
    act_ref[...] = gelu(jnp.transpose(x_ref[:, :rows]) * gain + shift)
    head = act_ref[:EDGE]
    tail = gelu(jnp.transpose(x_ref[:, length - LANES :])[LANES - EDGE :] * gain + shift)
    odd = lax.axis_index("seq") % 2 == 1
    head_ref[...] = head
    inner_ref[...] = jnp.where(odd, head, tail)
    outer_ref[...] = jnp.where(odd, tail, head)
    store_taps(hi_ref, lo_ref, act_ref, 2)
    for tap, copy in enumerate(copies):
        copy.wait()
        if tap + ahead < KW:
            copies[tap + ahead].start()
        split_tap(tap, w_ref.at[tap], far_hi, far_lo)


def opening(features, gain, shift, weight, rows):
    channels, length = features.shape
    outs = weight.shape[2]
    depth = KW * channels
    stack, split = bf16(padded(rows), depth), bf16(depth, outs // 2)
    span = -(-(padded(rows) + 6) // LANES) * LANES
    return pl.pallas_call(
        opening_kernel,
        in_specs=[IN_HBM] * 4,
        out_specs=[VECTORS] * 7,
        out_shape=[stack] * 2 + [f32(EDGE, channels)] * 3 + [split] * 2,
        scratch_shapes=[
            pltpu.VMEM((channels, length), jnp.float32),
            pltpu.VMEM((channels,), jnp.float32),
            pltpu.VMEM((channels,), jnp.float32),
            pltpu.VMEM((span, channels), jnp.float32),
            pltpu.VMEM((KW, channels, outs // 2), jnp.float32),
            pltpu.SemaphoreType.DMA((3,)),
            pltpu.SemaphoreType.DMA((KW,)),
        ],
        compiler_params=pltpu.CompilerParams(vmem_limit_bytes=10 * 1024 * 1024),
        cost_estimate=cost(LIGHT),
        name="opening",
    )(*map(in_hbm, (gain, shift, features, weight)))


def first_b_kernel(x_ref, gain_ref, shift_ref, head_ref, inner_ref, outer_ref, hi_ref, lo_ref, act_ref, *, chunk):
    gain, shift = gain_ref[...][None], shift_ref[...][None]
    length = x_ref.shape[1]
    base = (chunk + 2) // LANES * LANES
    top = length - base
    act_ref[:top] = gelu(jnp.transpose(x_ref[:, base:]) * gain + shift)
    odd = lax.axis_index("seq") % 2 == 1
    inner, outer = inner_ref[...], outer_ref[...]
    left = jnp.where(odd, inner, outer)
    right = jnp.where(odd, outer, inner)
    act_ref[top : top + 6] = right[:6]
    act_ref[top + 6 : top + 12] = left[2:]
    act_ref[top + 12 : top + 18] = head_ref[:6]
    act_ref[top + 18 :] = jnp.zeros((act_ref.shape[0] - top - 18, act_ref.shape[1]), jnp.float32)
    store_taps(hi_ref, lo_ref, act_ref, chunk + 2 - base)


def split_kernel(w_ref, hi_ref, lo_ref, *, far):
    outs = 2 * hi_ref.shape[1]
    for tap in range(KW):
        block = w_ref.at[tap]
        if w_ref.shape[2] == outs:
            block = block.at[:, half_columns(outs, far)]
        split_tap(tap, block, hi_ref, lo_ref)


def split_weight(weight, outs, far, flops=LIGHT):
    _, channels, _ = weight.shape
    return call(
        functools.partial(split_kernel, far=far), "split_far" if far else "split_own", [weight],
        [bf16(KW * channels, outs // 2)] * 2, flops=flops,
    )


def conv_kernel(hi_ref, lo_ref, whi_ref, wlo_ref, there_ref, here_ref):
    rows, owned = there_ref.shape
    for start in range(0, 2 * owned, 2 * LANES):
        cols = slice(start, start + 2 * LANES)
        hi, weight_hi = hi_ref[...], whi_ref[:, cols]
        total = jnp.dot(hi, weight_hi, preferred_element_type=jnp.float32)
        total += jnp.dot(lo_ref[...], weight_hi, preferred_element_type=jnp.float32)
        total += jnp.dot(hi, wlo_ref[:, cols], preferred_element_type=jnp.float32)
        for part in range(2):
            at = start + part * LANES
            values = total[:rows, part * LANES : (part + 1) * LANES]
            if at < owned:
                there_ref[:, at : at + LANES] = values
            else:
                here_ref[:, at - owned : at - owned + LANES] = values


def conv(stack, weight, rows, flops=LIGHT):
    owned = weight[0].shape[1] // 2
    depth = weight[0].shape[0]
    return call(
        conv_kernel, "conv", [*stack, *weight], [f32(rows, owned)] * 2, flops=flops
    )


def add_kernel(a_ref, b_ref, out_ref):
    out_ref[...] = a_ref[...] + b_ref[...]


def added(a, b):
    return call(add_kernel, "added", [a, b], [f32(*a.shape)])[0]


def put_sum(sum_ref, *refs):
    for j in range(sum_ref.shape[0]):
        cols = slice(j * LANES, (j + 1) * LANES)
        sum_ref[j] = sum(ref[:, cols] for ref in refs)


def pool_rows(sum_ref):
    blocks, rows, _ = sum_ref.shape
    return jnp.concatenate(
        [
            jnp.maximum(
                sum_ref[j, pl.ds(0, rows // 2, stride=2)], sum_ref[j, pl.ds(1, rows // 2, stride=2)]
            )
            for j in range(blocks)
        ],
        axis=1,
    )


def second_c_kernel(a_ref, b_ref, c_ref, gain_ref, shift_ref, hi_ref, lo_ref, ends_ref, sum_ref, act_ref):
    put_sum(sum_ref, a_ref, b_ref, c_ref)
    rows = a_ref.shape[0] // 2
    act_ref[:rows] = gelu(pool_rows(sum_ref) * gain_ref[...][None] + shift_ref[...][None])
    act_ref[rows:] = jnp.zeros((act_ref.shape[0] - rows, act_ref.shape[1]), jnp.float32)
    ends_ref[:4] = act_ref[:4]
    ends_ref[4:] = act_ref[rows - 4 : rows]
    store_taps(hi_ref, lo_ref, act_ref, 0)


def second_d_kernel(a_ref, b_ref, c_ref, gain_ref, shift_ref, ends_ref, hi_ref, lo_ref, sum_ref, act_ref):
    put_sum(sum_ref, a_ref, b_ref, c_ref)
    active = gelu(pool_rows(sum_ref) * gain_ref[...][None] + shift_ref[...][None])
    row = lax.broadcasted_iota(jnp.int32, active.shape, 0)
    main = active.shape[0] - 8
    seq = lax.axis_index("seq")
    ends = lax.axis_size("seq") - 1
    beyond = (row >= main - 2) & (row < main) & (seq == ends)
    before = (row >= main + 2) & (row < main + 4) & (seq == 0)
    active = jnp.where(beyond | before, 0.0, active)
    act_ref[:4] = ends_ref[4:]
    act_ref[4 : main + 4] = active[:main]
    act_ref[main + 4 : main + 8] = active[main + 2 : main + 6]
    act_ref[main + 8 : main + 12] = ends_ref[:4]
    act_ref[main + 12 :] = jnp.zeros((act_ref.shape[0] - main - 12, act_ref.shape[1]), jnp.float32)
    store_taps(hi_ref, lo_ref, act_ref, 0)


def pieces_kernel(*refs):
    ins, outs, (c_ref, d_ref, all_ref) = refs[:4], refs[4:-3], refs[-3:]
    put_sum(c_ref, *ins[:2])
    put_sum(d_ref, *ins[2:])
    pooled_d = pool_rows(d_ref)
    rows_c = ins[0].shape[0] // 2
    main = all_ref.shape[0] - 2 - rows_c
    all_ref[:2] = pooled_d[main + 2 : main + 4]
    all_ref[2 : 2 + rows_c] = pool_rows(c_ref)
    all_ref[2 + rows_c :] = pooled_d[:main]
    part = all_ref.shape[1] // GROUP
    turned = jnp.transpose(all_ref[...])
    member = lax.axis_index("seq") % GROUP
    for r in range(GROUP):
        for d in range(GROUP):
            @pl.when(member == r ^ d)
            def _():
                outs[d][...] = turned[r * part : (r + 1) * part]


def join_kernel(*refs):
    ins, out_ref = refs[:-1], refs[-1]
    width = ins[0].shape[1]
    member = lax.axis_index("seq") % GROUP
    for d, ref in enumerate(ins):
        out_ref[0, :, pl.ds(pl.multiple_of((member ^ d) * width, LANES), width)] = ref[...]


def after(values, *done):
    return lax.optimization_barrier((values, done))[0]


def body(features, gain_one, shift_one, wide_one, gain_two, shift_two, wide_two):
    n_seq = lax.axis_size("seq")
    one = [gain_one, shift_one]
    two = [gain_two, shift_two]
    channels, length = features.shape
    depth = KW * channels
    rows_a, rows_b, rows_c, rows_d = row_plan(length, CHUNK)

    outs = wide_one.shape[2]

    hi_a, lo_a, head, to_inner, to_outer, *far_one = opening(features, *one, wide_one, rows_a)
    there_a, here_a = conv((hi_a, lo_a), far_one, rows_a)
    own_one = split_weight(after(wide_one, there_a), outs, False)
    half_a = after(added(here_a, swapped(there_a, "ch", 1)), own_one)
    sum_a = swapped(half_a, "ch", 2)

    to_inner, to_outer = after((to_inner, to_outer), half_a)
    inner = lax.ppermute(to_inner, "seq", [(i, i ^ 1) for i in range(n_seq)])
    outer = lax.ppermute(
        to_outer, "seq", [p for i in range(1, n_seq - 1, 2) for p in ((i, i + 1), (i + 1, i))]
    )
    own_there_a, own_here_a = conv(after((hi_a, lo_a), half_a), own_one, rows_a, EARLY)
    own_a = own_here_a, swapped(own_there_a, "ch", 1)
    stack_b = call(
        functools.partial(first_b_kernel, chunk=CHUNK), "first_b",
        [after(features, own_here_a), *one, head, inner, outer],
        [bf16(padded(rows_b), depth)] * 2, [(length - (CHUNK + 2) // LANES * LANES + 48, channels)], EARLY,
    )
    there_b, here_b = conv(stack_b, far_one, rows_b, EARLY)
    half_b = added(here_b, swapped(there_b, "ch", 1))
    far_two = split_weight(after(wide_two, there_b), outs, True, EARLY)
    half_b = after(half_b, far_two)
    sum_b = swapped(half_b, "ch", 2)

    own_there_b, own_here_b = conv(after(stack_b, half_b), own_one, rows_b)
    own_b = own_here_b, swapped(own_there_b, "ch", 1)

    *stack_c, ends = call(
        second_c_kernel, "second_c", [after(sum_a, own_here_b), *own_a, *two],
        [bf16(padded(rows_c), depth)] * 2 + [f32(8, channels)],
        [(channels // LANES, rows_a, LANES), (padded(rows_c) + 8, channels)],
    )
    there_c, here_c = conv(stack_c, far_two, rows_c)
    own_two = split_weight(after(wide_two, there_c), outs, False)
    half_c = added(here_c, swapped(there_c, "ch", 1))
    half_c = after(half_c, own_two)
    sum_c = swapped(half_c, "ch", 2)

    stack_d = call(
        second_d_kernel, "second_d", [after(sum_b, half_c), *own_b, *two, ends],
        [bf16(padded(rows_d), depth)] * 2,
        [(channels // LANES, rows_b, LANES), (padded(rows_d) + 8, channels)], MIDDLE,
    )
    there_d, here_d = conv(stack_d, far_two, rows_d, MIDDLE)
    half_d = added(here_d, swapped(there_d, "ch", 1))
    own_there_c, own_here_c = conv(after(stack_c, there_d), own_two, rows_c, MIDDLE)
    half_d = after(half_d, own_here_c)
    sum_d = swapped(half_d, "ch", 2)
    own_there_d, own_here_d = conv(after(stack_d, half_d, sum_c), own_two, rows_d)
    here_d = call(add_kernel, "added", [sum_d, own_here_d], [f32(*sum_d.shape)], flops=HEAVY)[0]
    own_c = added(own_here_c, swapped(own_there_c, "ch", 1))
    last_d = after(swapped(own_there_d, "ch", 1), here_d)

    quarter = length // 4
    pieces = call(
        pieces_kernel, "pieces", [sum_c, own_c, here_d, last_d],
        [f32(channels // GROUP, quarter)] * GROUP,
        [(channels // LANES, rows_c, LANES), (channels // LANES, rows_d, LANES), (quarter, channels)],
    )
    blocks = [pieces[0]] + [swapped(pieces[d], "seq", d) for d in range(1, GROUP)]
    shape = jax.ShapeDtypeStruct((1, channels // GROUP, GROUP * quarter), jnp.float32)
    return call(join_kernel, "join", blocks, [shape])[0]


def solution(mesh):
    return jax.shard_map(
        body,
        mesh=mesh,
        in_specs=(
            P("ch", "seq"),
            P("ch"),
            P("ch"),
            P(None, "ch", None),
            P("ch"),
            P("ch"),
            P(None, "ch", None),
        ),
        out_specs=P("seq", "ch", None),
        check_vma=False,
    )
```

```python
import functools

import jax
import jax.numpy as jnp
from jax import lax
from jax.experimental import pallas as pl
from jax.experimental.pallas import tpu as pltpu
from jax.sharding import PartitionSpec as P

KW = 5
GROUP = 4
EDGE = 8
CHUNK = 296
LANES = 128
VMEM_LIMIT = 2 * 1024 * 1024
VECTORS = pl.BlockSpec(memory_space=pltpu.VMEM)
IN_HBM = pl.BlockSpec(memory_space=pltpu.HBM)
LIGHT = 1_000_000_000
MIDDLE = 10 * LIGHT
EARLY = 30 * LIGHT
HEAVY = 30 * LIGHT


def f32(*shape):
    return jax.ShapeDtypeStruct(shape, jnp.float32)


def bf16(*shape):
    return jax.ShapeDtypeStruct(shape, jnp.bfloat16)


def in_hbm(array):
    return pltpu.with_memory_space_constraint(array, pltpu.HBM)


def cost(flops):
    return pl.CostEstimate(flops=flops, transcendentals=0, bytes_accessed=0)


def call(kernel, name, args, outs, scratch=(), flops=LIGHT):
    return pl.pallas_call(
        kernel,
        in_specs=[VECTORS] * len(args),
        out_specs=[VECTORS] * len(outs),
        out_shape=list(outs),
        scratch_shapes=[pltpu.VMEM(shape, jnp.float32) for shape in scratch],
        compiler_params=pltpu.CompilerParams(vmem_limit_bytes=VMEM_LIMIT),
        cost_estimate=cost(flops),
        name=name,
    )(*args)


def swapped(block, axis, bit):
    count = lax.axis_size(axis)
    return lax.ppermute(block, axis, [(i, i ^ bit) for i in range(count)])


def gelu(values):
    return 0.5 * values * (1.0 + lax.erf(values * (0.5**0.5)))


def store_taps(hi_ref, lo_ref, act_ref, start):
    rows, channels = hi_ref.shape[0], act_ref.shape[1]
    for tap in range(KW):
        values = act_ref[pl.ds(start + tap, rows)]
        hi = values.astype(jnp.bfloat16)
        cols = slice(tap * channels, (tap + 1) * channels)
        hi_ref[:, cols] = hi
        lo_ref[:, cols] = (values - hi.astype(jnp.float32)).astype(jnp.bfloat16)


def row_plan(length, chunk):
    return chunk, length - chunk + 16, chunk // 2 - 4, (length - chunk) // 2 + 12


def padded(rows):
    return -(-rows // 16) * 16


def half_columns(outs, far):
    high = lax.axis_index("ch") // 2
    return pl.ds(pl.multiple_of((1 - high if far else high) * (outs // 2), LANES), outs // 2)


def split_tap(tap, w_ref, hi_ref, lo_ref):
    channels, owned = w_ref.shape[0], w_ref.shape[1] // 2
    core = lax.axis_index("ch") % 2
    for half, owner in enumerate((1 - core, core)):
        weight = w_ref[:, pl.ds(pl.multiple_of(owner * owned, LANES), owned)]
        hi = weight.astype(jnp.bfloat16)
        place = (slice(tap * channels, (tap + 1) * channels), slice(half * owned, (half + 1) * owned))
        hi_ref[place] = hi
        lo_ref[place] = (weight - hi.astype(jnp.float32)).astype(jnp.bfloat16)


def opening_kernel(gain_hbm, shift_hbm, x_hbm, w_hbm, hi_ref, lo_ref, head_ref, inner_ref, outer_ref, far_hi, far_lo,
                                      x_ref, gain_ref, shift_ref, act_ref, w_ref, x_sem, w_sem):
    length = x_ref.shape[1]
    gets = [
        pltpu.make_async_copy(src, dst, x_sem.at[i])
        for i, (src, dst) in enumerate(((gain_hbm, gain_ref), (shift_hbm, shift_ref), (x_hbm, x_ref)))
    ]
    cols = half_columns(w_hbm.shape[2], True)
    copies = [
        pltpu.make_async_copy(w_hbm.at[tap, :, cols], w_ref.at[tap], w_sem.at[tap]) for tap in range(KW)
    ]
    ahead = KW
    for copy in gets + copies[:ahead]:
        copy.start()
    for copy in gets:
        copy.wait()
    gain, shift = gain_ref[...][None], shift_ref[...][None]
    rows = act_ref.shape[0]
    act_ref[...] = gelu(jnp.transpose(x_ref[:, :rows]) * gain + shift)
    head = act_ref[:EDGE]
    tail = gelu(jnp.transpose(x_ref[:, length - LANES :])[LANES - EDGE :] * gain + shift)
    odd = lax.axis_index("seq") % 2 == 1
    head_ref[...] = head
    inner_ref[...] = jnp.where(odd, head, tail)
    outer_ref[...] = jnp.where(odd, tail, head)
    store_taps(hi_ref, lo_ref, act_ref, 2)
    for tap, copy in enumerate(copies):
        copy.wait()
        if tap + ahead < KW:
            copies[tap + ahead].start()
        split_tap(tap, w_ref.at[tap], far_hi, far_lo)


def opening(features, gain, shift, weight, rows):
    channels, length = features.shape
    outs = weight.shape[2]
    depth = KW * channels
    stack, split = bf16(padded(rows), depth), bf16(depth, outs // 2)
    span = -(-(padded(rows) + 6) // LANES) * LANES
    return pl.pallas_call(
        opening_kernel,
        in_specs=[IN_HBM] * 4,
        out_specs=[VECTORS] * 7,
        out_shape=[stack] * 2 + [f32(EDGE, channels)] * 3 + [split] * 2,
        scratch_shapes=[
            pltpu.VMEM((channels, length), jnp.float32),
            pltpu.VMEM((channels,), jnp.float32),
            pltpu.VMEM((channels,), jnp.float32),
            pltpu.VMEM((span, channels), jnp.float32),
            pltpu.VMEM((KW, channels, outs // 2), jnp.float32),
            pltpu.SemaphoreType.DMA((3,)),
            pltpu.SemaphoreType.DMA((KW,)),
        ],
        compiler_params=pltpu.CompilerParams(vmem_limit_bytes=10 * 1024 * 1024),
        cost_estimate=cost(LIGHT),
        name="opening",
    )(*map(in_hbm, (gain, shift, features, weight)))


def first_b_kernel(x_ref, gain_ref, shift_ref, head_ref, inner_ref, outer_ref, hi_ref, lo_ref, act_ref, *, chunk):
    gain, shift = gain_ref[...][None], shift_ref[...][None]
    length = x_ref.shape[1]
    base = (chunk + 2) // LANES * LANES
    top = length - base
    act_ref[:top] = gelu(jnp.transpose(x_ref[:, base:]) * gain + shift)
    odd = lax.axis_index("seq") % 2 == 1
    inner, outer = inner_ref[...], outer_ref[...]
    left = jnp.where(odd, inner, outer)
    right = jnp.where(odd, outer, inner)
    act_ref[top : top + 6] = right[:6]
    act_ref[top + 6 : top + 12] = left[2:]
    act_ref[top + 12 : top + 18] = head_ref[:6]
    act_ref[top + 18 :] = jnp.zeros((act_ref.shape[0] - top - 18, act_ref.shape[1]), jnp.float32)
    store_taps(hi_ref, lo_ref, act_ref, chunk + 2 - base)


def split_kernel(w_ref, hi_ref, lo_ref, *, far):
    outs = 2 * hi_ref.shape[1]
    for tap in range(KW):
        block = w_ref.at[tap]
        if w_ref.shape[2] == outs:
            block = block.at[:, half_columns(outs, far)]
        split_tap(tap, block, hi_ref, lo_ref)


def split_weight(weight, outs, far, flops=LIGHT):
    _, channels, _ = weight.shape
    return call(
        functools.partial(split_kernel, far=far), "split_far" if far else "split_own", [weight],
        [bf16(KW * channels, outs // 2)] * 2, flops=flops,
    )


def conv_kernel(hi_ref, lo_ref, whi_ref, wlo_ref, there_ref, here_ref):
    rows, owned = there_ref.shape
    for start in range(0, 2 * owned, 2 * LANES):
        cols = slice(start, start + 2 * LANES)
        hi, weight_hi = hi_ref[...], whi_ref[:, cols]
        total = jnp.dot(hi, weight_hi, preferred_element_type=jnp.float32)
        total += jnp.dot(lo_ref[...], weight_hi, preferred_element_type=jnp.float32)
        total += jnp.dot(hi, wlo_ref[:, cols], preferred_element_type=jnp.float32)
        for part in range(2):
            at = start + part * LANES
            values = total[:rows, part * LANES : (part + 1) * LANES]
            if at < owned:
                there_ref[:, at : at + LANES] = values
            else:
                here_ref[:, at - owned : at - owned + LANES] = values


def conv(stack, weight, rows, flops=LIGHT):
    owned = weight[0].shape[1] // 2
    depth = weight[0].shape[0]
    return call(
        conv_kernel, "conv", [*stack, *weight], [f32(rows, owned)] * 2, flops=flops
    )


def add_kernel(a_ref, b_ref, out_ref):
    out_ref[...] = a_ref[...] + b_ref[...]


def added(a, b):
    return call(add_kernel, "added", [a, b], [f32(*a.shape)])[0]


def put_sum(sum_ref, *refs):
    for j in range(sum_ref.shape[0]):
        cols = slice(j * LANES, (j + 1) * LANES)
        sum_ref[j] = sum(ref[:, cols] for ref in refs)


def pool_rows(sum_ref):
    blocks, rows, _ = sum_ref.shape
    return jnp.concatenate(
        [
            jnp.maximum(
                sum_ref[j, pl.ds(0, rows // 2, stride=2)], sum_ref[j, pl.ds(1, rows // 2, stride=2)]
            )
            for j in range(blocks)
        ],
        axis=1,
    )


def second_c_kernel(a_ref, b_ref, c_ref, gain_ref, shift_ref, hi_ref, lo_ref, ends_ref, sum_ref, act_ref):
    put_sum(sum_ref, a_ref, b_ref, c_ref)
    rows = a_ref.shape[0] // 2
    act_ref[:rows] = gelu(pool_rows(sum_ref) * gain_ref[...][None] + shift_ref[...][None])
    act_ref[rows:] = jnp.zeros((act_ref.shape[0] - rows, act_ref.shape[1]), jnp.float32)
    ends_ref[:4] = act_ref[:4]
    ends_ref[4:] = act_ref[rows - 4 : rows]
    store_taps(hi_ref, lo_ref, act_ref, 0)


def second_d_kernel(a_ref, b_ref, c_ref, gain_ref, shift_ref, ends_ref, hi_ref, lo_ref, sum_ref, act_ref):
    put_sum(sum_ref, a_ref, b_ref, c_ref)
    active = gelu(pool_rows(sum_ref) * gain_ref[...][None] + shift_ref[...][None])
    row = lax.broadcasted_iota(jnp.int32, active.shape, 0)
    main = active.shape[0] - 8
    seq = lax.axis_index("seq")
    ends = lax.axis_size("seq") - 1
    beyond = (row >= main - 2) & (row < main) & (seq == ends)
    before = (row >= main + 2) & (row < main + 4) & (seq == 0)
    active = jnp.where(beyond | before, 0.0, active)
    act_ref[:4] = ends_ref[4:]
    act_ref[4 : main + 4] = active[:main]
    act_ref[main + 4 : main + 8] = active[main + 2 : main + 6]
    act_ref[main + 8 : main + 12] = ends_ref[:4]
    act_ref[main + 12 :] = jnp.zeros((act_ref.shape[0] - main - 12, act_ref.shape[1]), jnp.float32)
    store_taps(hi_ref, lo_ref, act_ref, 0)


def pieces_kernel(*refs):
    ins, outs, (c_ref, d_ref, all_ref) = refs[:4], refs[4:-3], refs[-3:]
    put_sum(c_ref, *ins[:2])
    put_sum(d_ref, *ins[2:])
    pooled_d = pool_rows(d_ref)
    rows_c = ins[0].shape[0] // 2
    main = all_ref.shape[0] - 2 - rows_c
    all_ref[:2] = pooled_d[main + 2 : main + 4]
    all_ref[2 : 2 + rows_c] = pool_rows(c_ref)
    all_ref[2 + rows_c :] = pooled_d[:main]
    part = all_ref.shape[1] // GROUP
    turned = jnp.transpose(all_ref[...])
    member = lax.axis_index("seq") % GROUP
    for r in range(GROUP):
        for d in range(GROUP):
            @pl.when(member == r ^ d)
            def _():
                outs[d][...] = turned[r * part : (r + 1) * part]


def join_kernel(*refs):
    ins, out_ref = refs[:-1], refs[-1]
    width = ins[0].shape[1]
    member = lax.axis_index("seq") % GROUP
    for d, ref in enumerate(ins):
        out_ref[0, :, pl.ds(pl.multiple_of((member ^ d) * width, LANES), width)] = ref[...]


def after(values, *done):
    return lax.optimization_barrier((values, done))[0]


def body(features, gain_one, shift_one, wide_one, gain_two, shift_two, wide_two):
    n_seq = lax.axis_size("seq")
    one = [gain_one, shift_one]
    two = [gain_two, shift_two]
    channels, length = features.shape
    depth = KW * channels
    rows_a, rows_b, rows_c, rows_d = row_plan(length, CHUNK)

    outs = wide_one.shape[2]

    hi_a, lo_a, head, to_inner, to_outer, *far_one = opening(features, *one, wide_one, rows_a)
    there_a, here_a = conv((hi_a, lo_a), far_one, rows_a)
    own_one = split_weight(after(wide_one, there_a), outs, False)
    half_a = after(added(here_a, swapped(there_a, "ch", 1)), own_one)
    sum_a = swapped(half_a, "ch", 2)

    to_inner, to_outer = after((to_inner, to_outer), half_a)
    inner = lax.ppermute(to_inner, "seq", [(i, i ^ 1) for i in range(n_seq)])
    outer = lax.ppermute(
        to_outer, "seq", [p for i in range(1, n_seq - 1, 2) for p in ((i, i + 1), (i + 1, i))]
    )
    stack_b = call(
        functools.partial(first_b_kernel, chunk=CHUNK), "first_b",
        [after(features, half_a), *one, head, inner, outer],
        [bf16(padded(rows_b), depth)] * 2, [(length - (CHUNK + 2) // LANES * LANES + 48, channels)], EARLY,
    )
    there_b, here_b = conv(stack_b, far_one, rows_b, EARLY)
    own_there_a, own_here_a = conv(after((hi_a, lo_a), there_b), own_one, rows_a, EARLY)
    own_a = own_here_a, swapped(own_there_a, "ch", 1)
    half_b = after(added(here_b, swapped(there_b, "ch", 1)), own_here_a)
    sum_b = swapped(half_b, "ch", 2)

    own_there_b, own_here_b = conv(after(stack_b, half_b), own_one, rows_b)
    own_b = own_here_b, swapped(own_there_b, "ch", 1)
    far_two = split_weight(after(wide_two, own_here_b), outs, True)

    *stack_c, ends = call(
        second_c_kernel, "second_c", [after(sum_a, far_two), *own_a, *two],
        [bf16(padded(rows_c), depth)] * 2 + [f32(8, channels)],
        [(channels // LANES, rows_a, LANES), (padded(rows_c) + 8, channels)],
    )
    there_c, here_c = conv(stack_c, far_two, rows_c)
    own_two = split_weight(after(wide_two, there_c), outs, False)
    half_c = added(here_c, swapped(there_c, "ch", 1))
    half_c = after(half_c, own_two)
    sum_c = swapped(half_c, "ch", 2)

    stack_d = call(
        second_d_kernel, "second_d", [after(sum_b, half_c), *own_b, *two, ends],
        [bf16(padded(rows_d), depth)] * 2,
        [(channels // LANES, rows_b, LANES), (padded(rows_d) + 8, channels)], MIDDLE,
    )
    there_d, here_d = conv(stack_d, far_two, rows_d, MIDDLE)
    half_d = added(here_d, swapped(there_d, "ch", 1))
    own_there_c, own_here_c = conv(after(stack_c, there_d), own_two, rows_c, MIDDLE)
    half_d = after(half_d, own_here_c)
    sum_d = swapped(half_d, "ch", 2)
    own_there_d, own_here_d = conv(after(stack_d, half_d, sum_c), own_two, rows_d)
    here_d = call(add_kernel, "added", [sum_d, own_here_d], [f32(*sum_d.shape)], flops=HEAVY)[0]
    own_c = added(own_here_c, swapped(own_there_c, "ch", 1))
    last_d = after(swapped(own_there_d, "ch", 1), here_d)

    quarter = length // 4
    pieces = call(
        pieces_kernel, "pieces", [sum_c, own_c, here_d, last_d],
        [f32(channels // GROUP, quarter)] * GROUP,
        [(channels // LANES, rows_c, LANES), (channels // LANES, rows_d, LANES), (quarter, channels)],
    )
    blocks = [pieces[0]] + [swapped(pieces[d], "seq", d) for d in range(1, GROUP)]
    shape = jax.ShapeDtypeStruct((1, channels // GROUP, GROUP * quarter), jnp.float32)
    return call(join_kernel, "join", blocks, [shape])[0]


def solution(mesh):
    return jax.shard_map(
        body,
        mesh=mesh,
        in_specs=(
            P("ch", "seq"),
            P("ch"),
            P("ch"),
            P(None, "ch", None),
            P("ch"),
            P("ch"),
            P(None, "ch", None),
        ),
        out_specs=P("seq", "ch", None),
        check_vma=False,
    )
```
